512 devices in a mesh: blk: 64 (over z, x), uly: 8 (over y, core).
Axes of the slice: x: 4, y: 4, z: 16, core: 2. Of those that a mesh axis runs over, the one named last changes fastest.
Arguments:
- queries: bfloat16 [65536, 8192], P(('blk', 'uly'))
- keys: bfloat16 [65536, 1024], P(('blk', 'uly'))
- values: bfloat16 [65536, 1024], P(('blk', 'uly')), may hold values from -6 to 6
- chosen: int32 [128, 8, 2], replicated, may hold values from 0 to 126, as said below
Outputs:
- attended: bfloat16 [65536, 8192], P(('blk', 'uly'))
The draws below stay inside these ranges and needn't reach their ends.
Inputs may be any that keep to these rules, and one draw needn't show every extreme that they name: For attention block j and key-value head h, chosen[j, h, 0] and chosen[j, h, 1] differ; for j >= 2 both are below j; for j < 2 at least one is not below j. An id that is not below j selects nothing.
All inputs are finite; a program needn't handle non-finite values.
Results may differ from the reference program's by a relative error of at most 0.0046.
Values may be sent and summed in bfloat16 or wider, within the bound.
A program may use at most 64 MiB of HBM per device.

```python
import jax
import jax.numpy as jnp
from jax import lax

BS = 512
HD = 128
GROUP = 8
KVH = 8
TOKENS = 65536
NBLOCKS = 128


def draw_queries(key, part):
    shape = (TOKENS, KVH, GROUP, HD)
    own_key = jax.random.fold_in(key, 1)
    base = jnp.clip(jax.random.normal(own_key, shape, jnp.float32), -6.0, 6.0)
    return base.reshape(TOKENS, KVH * GROUP * HD).astype(jnp.bfloat16)


def draw_keys(key, part):
    shape = (TOKENS, KVH, HD)
    own_key = jax.random.fold_in(key, 2)
    base = jnp.clip(jax.random.normal(own_key, shape, jnp.float32), -6.0, 6.0)
    return base.reshape(TOKENS, KVH * HD).astype(jnp.bfloat16)


def draw_chosen(key, part):
    block = jnp.arange(NBLOCKS, dtype=jnp.int32)[:, None]
    heads = jnp.arange(KVH, dtype=jnp.int32)[None, :]
    first = jax.random.randint(jax.random.fold_in(key, 5), (NBLOCKS, KVH), 0, jnp.maximum(block, 1))
    first = jnp.where((block == NBLOCKS - 1) & (heads == 0), NBLOCKS - 2, first).astype(jnp.int32)
    other = jax.random.randint(jax.random.fold_in(key, 6), (NBLOCKS, KVH), 0, jnp.maximum(block - 1, 1))
    second = other + (other >= first).astype(jnp.int32)
    return jnp.stack([first, second], axis=-1).astype(jnp.int32)


def steps_of(rng, shape, cuts, low, largest):
    def one(dim, parts):
        draws = jax.random.uniform(jax.random.fold_in(jax.random.fold_in(rng, 6), dim), (parts,), jnp.float32, low / len(cuts), largest / len(cuts))
        return jnp.repeat(jnp.exp(draws), shape[dim] // parts).reshape((-1,) + (1,) * (len(shape) - dim - 1))

    loudness = one(*cuts[0])
    for cut in cuts[1:]:
        loudness = loudness * one(*cut)
    return loudness


def gaussian(key, extent, deviation, reach, shards=(), kind=jnp.bfloat16):
    loudness = steps_of(key, extent, shards, -0.22, 0.18) if shards else 1.0
    drawn = jax.random.normal(key, extent, jnp.float32) * deviation * loudness
    return jnp.minimum(jnp.maximum(drawn, -reach), reach).astype(kind)


def setup_inputs(seed: int = 0) -> dict:
    splits = jax.random.split(jax.random.key(seed), 5)
    queries = draw_queries(jax.random.fold_in(splits[4], 71), 0)
    keys = draw_keys(jax.random.fold_in(splits[4], 71), 0)
    values = gaussian(splits[2], (TOKENS, KVH * HD), 1.0, 6.0, ((0, 512),))
    chosen = draw_chosen(jax.random.fold_in(splits[4], 71), 0)
    return dict(queries=queries, keys=keys, values=values, chosen=chosen)


def reference(queries, keys, values, chosen):
    scale = HD ** -0.5
    q_blocks = queries.reshape(NBLOCKS, BS, KVH, GROUP, HD)
    key_table = jnp.transpose(keys.reshape(NBLOCKS, BS, KVH, HD), (2, 0, 1, 3))
    value_table = jnp.transpose(values.reshape(NBLOCKS, BS, KVH, HD), (2, 0, 1, 3))
    causal = jnp.arange(BS, dtype=jnp.int32)[None, :] <= jnp.arange(BS, dtype=jnp.int32)[:, None]
    head_rows = jnp.arange(KVH, dtype=jnp.int32)[:, None]

    def one_block(block):
        query_rows = q_blocks[block].astype(jnp.float32)
        picks = chosen[block]
        key_rows = jnp.concatenate([key_table[:, block][:, None], key_table[head_rows, picks]], axis=1)
        value_rows = jnp.concatenate([value_table[:, block][:, None], value_table[head_rows, picks]], axis=1)
        key_rows = key_rows.reshape(KVH, 3 * BS, HD).astype(jnp.float32)
        value_rows = value_rows.reshape(KVH, 3 * BS, HD).astype(jnp.float32)
        scores = jnp.einsum("tkgd,ksd->kgts", query_rows, key_rows) * scale
        usable = picks < block
        routed = jnp.broadcast_to(usable[:, None, :, None], (KVH, BS, 2, BS)).reshape(KVH, BS, 2 * BS)
        own = jnp.broadcast_to(causal[None], (KVH, BS, BS))
        allowed = jnp.concatenate([own, routed], axis=2)[:, None]
        scores = jnp.where(allowed, scores, -jnp.inf)
        top = jnp.max(scores, axis=-1, keepdims=True)
        weights = jnp.exp(scores - top)
        total = jnp.sum(weights, axis=-1, keepdims=True)
        rounded = lax.optimization_barrier(weights.astype(jnp.bfloat16)).astype(jnp.float32)
        summed = jnp.einsum("kgts,ksd->tkgd", rounded, value_rows)
        return (summed / jnp.transpose(total, (2, 0, 1, 3))).astype(jnp.bfloat16)

    outputs = lax.map(one_block, jnp.arange(NBLOCKS, dtype=jnp.int32))
    return outputs.reshape(TOKENS, KVH * GROUP * HD)
```

```python
import functools

import jax
import jax.numpy as jnp
from jax import lax
from jax.experimental import pallas as pl
from jax.experimental.pallas import tpu as pltpu
from jax.sharding import PartitionSpec as P

BS = 512
HD = 128
GROUP = 8
LOG2E = 1.4426950408889634
NEG = -3.0e38
MESH = pl.DeviceIdType.MESH


def kernel(
    blk_n, uly_n, x_n,
    q_ref, k_ref, v_ref, chosen_ref,
    out_ref,
    qh, kv, table, stage, routed, own_acc, own_top, outh,
    kv_send, kv_recv, q_send, q_recv, spread_send, spread_recv, ask_send, ask_recv, out_send, out_recv, self_sem,
):
    rank = lax.axis_index("blk")
    head = lax.axis_index("uly")
    tok = q_ref.shape[0]
    width = GROUP * HD
    span = uly_n * tok
    here = span // BS
    per = BS // tok
    rows = 2 * BS // blk_n
    half_g = GROUP // 2
    z_n = blk_n // x_n
    factor = HD ** (-0.5) * LOG2E
    flip = lax.rem(head, 2)

    def blk_peer(i):
        dx = lax.rem(i, x_n)
        k = lax.div(i, x_n)
        step = lax.div(k + 1, 2)
        dz = jnp.where(lax.rem(k, 2) == 1, step, z_n - step)
        z = lax.rem(lax.div(rank, x_n) + dz, z_n)
        x = lax.rem(lax.rem(rank, x_n) + dx, x_n)
        return z * x_n + x

    def uly_peer(i):
        return lax.rem(head + i, uly_n)

    barrier = pltpu.get_barrier_semaphore()

    def greet_uly(i, c):
        pl.semaphore_signal(barrier, inc=1, device_id=(rank, uly_peer(i)), device_id_type=MESH)
        return c

    def greet_blk(i, c):
        pl.semaphore_signal(barrier, inc=1, device_id=(blk_peer(i), head), device_id_type=MESH)
        return c

    lax.fori_loop(1, uly_n, greet_uly, 0)
    lax.fori_loop(1, blk_n, greet_blk, 0)
    pl.semaphore_wait(barrier, uly_n + blk_n - 2)

    my_block = lax.div(head, per)
    my_row = pl.multiple_of(lax.rem(head, per) * tok, tok)
    my_rows = pl.ds(my_row, tok)
    my_rows_v = pl.ds(pl.multiple_of(my_row + BS, tok), tok)

    def send_kv(i, c):
        p = uly_peer(i)
        cols = pl.ds(pl.multiple_of(p * HD, HD), HD)
        for src, dst_rows in ((k_ref, my_rows), (v_ref, my_rows_v)):
            pltpu.make_async_remote_copy(
                src.at[:, cols], kv.at[my_block, dst_rows, :], kv_send, kv_recv,
                device_id=(rank, p), device_id_type=MESH,
            ).start()
        return c

    lax.fori_loop(1, uly_n, send_kv, 0)
    own_cols = pl.ds(pl.multiple_of(head * HD, HD), HD)
    own_k = pltpu.make_async_copy(k_ref.at[:, own_cols], kv.at[my_block, my_rows, :], self_sem.at[0])
    own_v = pltpu.make_async_copy(v_ref.at[:, own_cols], kv.at[my_block, my_rows_v, :], self_sem.at[1])
    own_k.start()
    own_v.start()

    def send_q(i, c):
        p = uly_peer(i)
        pltpu.make_async_remote_copy(
            q_ref.at[:, pl.ds(pl.multiple_of(p * width, width), width)],
            qh.at[pl.ds(pl.multiple_of(head * tok, tok), tok), :],
            q_send, q_recv, device_id=(rank, p), device_id_type=MESH,
        ).start()
        return c

    lax.fori_loop(1, uly_n, send_q, 0)
    own_q = pltpu.make_async_copy(
        q_ref.at[:, pl.ds(pl.multiple_of(head * width, width), width)],
        qh.at[pl.ds(pl.multiple_of(head * tok, tok), tok), :], self_sem.at[2])
    own_q.start()

    def wait_bytes(ref, sem):
        pltpu.make_async_copy(ref, ref, sem).wait()

    own_k.wait()
    own_v.wait()
    kv_part = kv.at[:, pl.ds(0, 2 * BS * (uly_n - 1) // uly_n), :]
    wait_bytes(kv_part, kv_recv)

    def send_spread(i, c):
        p = blk_peer(i)
        pltpu.make_async_remote_copy(
            kv.at[:, pl.ds(pl.multiple_of(p * rows, rows), rows), :],
            table.at[pl.ds(rank * here, here)],
            spread_send, spread_recv, device_id=(p, head), device_id_type=MESH,
        ).start()
        return c

    lax.fori_loop(1, blk_n, send_spread, 0)
    table[pl.ds(rank * here, here)] = kv[:, pl.ds(pl.multiple_of(rank * rows, rows), rows), :]
    spread_part = table.at[pl.ds(0, here * (blk_n - 1))]
    wait_bytes(spread_part, spread_recv)

    my_share = pl.ds(pl.multiple_of(rank * rows, rows), rows)

    def pick(half, p):
        block = p * here + lax.rem(half + flip, 2)
        for s in range(2):
            stage[half, p, s] = table[chosen_ref[(block * uly_n + head) * 2 + s]]

    def send_ask(n, c):
        half = lax.div(n, blk_n - 1)
        p = blk_peer(lax.rem(n, blk_n - 1) + 1)
        pick(half, p)
        pltpu.make_async_remote_copy(
            stage.at[half, p], routed.at[half, :, my_share, :],
            ask_send, ask_recv.at[half], device_id=(p, head), device_id_type=MESH,
        ).start()
        return c

    lax.fori_loop(0, here * (blk_n - 1), send_ask, 0)
    for half in range(here):
        pick(half, rank)
        routed[half, :, my_share, :] = stage[half, rank]

    own_q.wait()
    wait_bytes(qh.at[pl.ds(0, span - tok), :], q_recv)

    def queries(row, gh):
        return jnp.concatenate(
            [qh[pl.ds(row, tok), pl.ds(pl.multiple_of((gh * half_g + g) * HD, HD), HD)] for g in range(half_g)], axis=0)

    contract = (((1,), (1,)), ((), ()))
    ones = jnp.ones((BS, HD), jnp.bfloat16)

    def own_step(i, c):
        b = lax.div(i, 2)
        gh = lax.rem(i, 2)
        for part in range(per):
            q = queries(pl.multiple_of(b * BS + part * tok, tok), gh)
            n = (part + 1) * tok
            scores = lax.dot_general(q, kv[b, 0:n, :], contract, preferred_element_type=jnp.float32)
            r = lax.rem(lax.broadcasted_iota(jnp.int32, (half_g * tok, tok), 0), tok)
            k = lax.broadcasted_iota(jnp.int32, (half_g * tok, tok), 1)
            diag = jnp.where(k <= r, scores[:, n - tok:], -jnp.inf)
            if part:
                scores = jnp.concatenate([scores[:, : n - tok], diag], axis=1)
            else:
                scores = diag
            top = jnp.max(scores, axis=1, keepdims=True)
            weights = jnp.exp2(scores * factor - top * factor).astype(jnp.bfloat16)
            v1 = jnp.concatenate([kv[b, BS:BS + n, :], ones[:n]], axis=1)
            own_acc[b, part, gh] = jnp.dot(weights, v1, preferred_element_type=jnp.float32)
            own_top[b, part, gh] = jnp.broadcast_to(top, (half_g * tok, HD))
        return c

    lax.fori_loop(0, here * 2, own_step, 0)

    def routed_step(n, c):
        half = lax.div(n, per)
        b = lax.rem(half + flip, 2)
        part = lax.rem(n + lax.div(head, 2), per)

        @pl.when(lax.rem(n, per) == 0)
        def _():
            wait_bytes(spread_part, ask_recv.at[half])

        block = rank * here + b
        usable = [chosen_ref[(block * uly_n + head) * 2 + s] < block for s in range(2)]
        row = pl.multiple_of(b * BS + part * tok, tok)

        def group_step(gh, c):
            q = queries(row, gh)
            before = own_top[b, part, gh][:, 0:1]
            scores = [
                lax.dot_general(q, routed[half, s, 0:BS, :], contract, preferred_element_type=jnp.float32)
                for s in range(2)
            ]
            top = before
            for s in range(2):
                top = jnp.maximum(top, jnp.where(usable[s], jnp.max(scores[s], axis=1, keepdims=True), NEG))
            acc = own_acc[b, part, gh] * jnp.exp2((before - top) * factor)
            for s in range(2):
                shift = jnp.where(usable[s], top * factor, jnp.inf)
                weights = jnp.exp2(scores[s] * factor - shift).astype(jnp.bfloat16)
                v1 = jnp.concatenate([routed[half, s, BS:, :], ones], axis=1)
                acc = acc + jnp.dot(weights, v1, preferred_element_type=jnp.float32)
            result = (acc[:, :HD] / acc[:, HD:]).astype(jnp.bfloat16)
            for g in range(half_g):
                outh[pl.ds(row, tok), pl.ds(pl.multiple_of((gh * half_g + g) * HD, HD), HD)] = (
                    result[g * tok:(g + 1) * tok])
            return c

        lax.fori_loop(0, 2, group_step, 0)
        p = b * per + part
        src = outh.at[pl.ds(row, tok), :]
        dst = out_ref.at[:, pl.ds(pl.multiple_of(head * width, width), width)]

        @pl.when(p != head)
        def _():
            pltpu.make_async_remote_copy(
                src, dst, out_send, out_recv, device_id=(rank, p), device_id_type=MESH).start()

        @pl.when(p == head)
        def _():
            pltpu.make_async_copy(src, dst, self_sem.at[3]).start()

        return c

    lax.fori_loop(0, here * per, routed_step, 0)

    pltpu.make_async_copy(
        outh.at[pl.ds(0, tok), :], out_ref.at[:, pl.ds(0, width)], self_sem.at[3]).wait()
    wait_bytes(kv_part, kv_send)
    wait_bytes(qh.at[pl.ds(0, span - tok), :], q_send)
    wait_bytes(spread_part, spread_send)
    wait_bytes(stage.at[:, pl.ds(0, blk_n - 1)], ask_send)
    wait_bytes(qh.at[pl.ds(0, span - tok), :], out_send)
    wait_bytes(qh.at[pl.ds(0, span - tok), :], out_recv)


def solution(mesh):
    blk_n, uly_n = mesh.shape["blk"], mesh.shape["uly"]
    x_n = 4 if blk_n % 4 == 0 else 1

    def local(queries, keys, values, chosen):
        tok = queries.shape[0]
        span = tok * uly_n
        here = span // BS
        rows = 2 * BS // blk_n
        per = BS // tok
        bf = jnp.bfloat16
        any_spec = pl.BlockSpec(memory_space=pl.ANY)
        dma = pltpu.SemaphoreType.DMA
        return pl.pallas_call(
            functools.partial(kernel, blk_n, uly_n, x_n),
            out_shape=jax.ShapeDtypeStruct(queries.shape, bf),
            in_specs=[any_spec, any_spec, any_spec, pl.BlockSpec(memory_space=pltpu.SMEM)],
            out_specs=any_spec,
            scratch_shapes=[
                pltpu.VMEM((span, GROUP * HD), bf),
                pltpu.VMEM((here, 2 * BS, HD), bf),
                pltpu.VMEM((blk_n * here, rows, HD), bf),
                pltpu.VMEM((here, blk_n, 2, rows, HD), bf),
                pltpu.VMEM((here, 2, 2 * BS, HD), bf),
                pltpu.VMEM((here, per, 2, GROUP // 2 * tok, 2 * HD), jnp.float32),
                pltpu.VMEM((here, per, 2, GROUP // 2 * tok, HD), jnp.float32),
                pltpu.VMEM((span, GROUP * HD), bf),
                dma, dma, dma, dma, dma, dma, dma, dma((here,)), dma, dma, dma((4,)),
            ],
            compiler_params=pltpu.CompilerParams(
                collective_id=0, has_side_effects=True, vmem_limit_bytes=56 * 2**20),
        )(queries, keys, values, chosen.reshape(-1))

    placed = P(("blk", "uly"), None)
    return jax.shard_map(
        local, mesh=mesh, in_specs=(placed, placed, placed, P()), out_specs=placed, check_vma=False)
```

```python
import functools

import jax
import jax.numpy as jnp
from jax import lax
from jax.experimental import pallas as pl
from jax.experimental.pallas import tpu as pltpu
from jax.sharding import PartitionSpec as P

BS = 512
HD = 128
GROUP = 8
LOG2E = 1.4426950408889634
NEG = -3.0e38
MESH = pl.DeviceIdType.MESH


def kernel(
    blk_n, uly_n, x_n,
    q_ref, k_ref, v_ref, chosen_ref,
    out_ref,
    qh, kv, table, stage, routed, own_acc, own_top, outh,
    kv_send, kv_recv, q_send, q_recv, spread_send, spread_recv, ask_send, ask_recv, out_send, out_recv, self_sem, turn,
):
    rank = lax.axis_index("blk")
    head = lax.axis_index("uly")
    tok = q_ref.shape[0]
    width = GROUP * HD
    span = uly_n * tok
    here = span // BS
    per = BS // tok
    rows = 2 * BS // blk_n
    half_g = GROUP // 2
    z_n = blk_n // x_n
    factor = HD ** (-0.5) * LOG2E
    home = lax.div(head, per)
    seat = lax.rem(head, per)

    def own_last(half):
        return jnp.where(half == here - 1, home, here - 1 - home)

    def blk_peer(i):
        i = lax.rem(blk_n - i, blk_n)
        dx = lax.rem(i, x_n)
        k = lax.div(i, x_n)
        step = lax.div(k + 1, 2)
        dz = jnp.where(lax.rem(k, 2) == 1, step, z_n - step)
        z = lax.rem(lax.div(rank, x_n) + dz, z_n)
        x = lax.rem(lax.rem(rank, x_n) + dx, x_n)
        return z * x_n + x

    def uly_peer(i):
        return lax.rem(head + i, uly_n)

    barrier = pltpu.get_barrier_semaphore()

    def greet_uly(i, c):
        pl.semaphore_signal(barrier, inc=1, device_id=(rank, uly_peer(i)), device_id_type=MESH)
        return c

    def greet_blk(i, c):
        pl.semaphore_signal(barrier, inc=1, device_id=(blk_peer(i), head), device_id_type=MESH)
        return c

    lax.fori_loop(1, uly_n, greet_uly, 0)
    lax.fori_loop(1, blk_n, greet_blk, 0)
    pl.semaphore_wait(barrier, uly_n + blk_n - 2)

    my_block = home
    my_row = pl.multiple_of(seat * tok, tok)
    my_rows = pl.ds(my_row, tok)
    my_rows_v = pl.ds(pl.multiple_of(my_row + BS, tok), tok)

    def send_kv(i, c):
        p = 2 * lax.rem(lax.div(head, 2) + lax.rem(i, uly_n // 2), uly_n // 2) + lax.div(i, uly_n // 2)
        cols = pl.ds(pl.multiple_of(p * HD, HD), HD)

        @pl.when(p != head)
        def _():
            for src, dst_rows in ((k_ref, my_rows), (v_ref, my_rows_v)):
                pltpu.make_async_remote_copy(
                    src.at[:, cols], kv.at[my_block, dst_rows, :], kv_send, kv_recv,
                    device_id=(rank, p), device_id_type=MESH,
                ).start()

        return c

    lax.fori_loop(0, uly_n, send_kv, 0)
    own_cols = pl.ds(pl.multiple_of(head * HD, HD), HD)
    own_k = pltpu.make_async_copy(k_ref.at[:, own_cols], kv.at[my_block, my_rows, :], self_sem.at[0])
    own_v = pltpu.make_async_copy(v_ref.at[:, own_cols], kv.at[my_block, my_rows_v, :], self_sem.at[1])
    own_k.start()
    own_v.start()

    def send_q(i, c):
        p = uly_peer(i)
        pltpu.make_async_remote_copy(
            q_ref.at[:, pl.ds(pl.multiple_of(p * width, width), width)],
            qh.at[pl.ds(pl.multiple_of(head * tok, tok), tok), :],
            q_send, q_recv, device_id=(rank, p), device_id_type=MESH,
        ).start()
        return c

    lax.fori_loop(1, uly_n, send_q, 0)
    own_q = pltpu.make_async_copy(
        q_ref.at[:, pl.ds(pl.multiple_of(head * width, width), width)],
        qh.at[pl.ds(pl.multiple_of(head * tok, tok), tok), :], self_sem.at[2])
    own_q.start()

    def wait_bytes(ref, sem):
        pltpu.make_async_copy(ref, ref, sem).wait()

    own_k.wait()
    own_v.wait()
    kv_part = kv.at[:, pl.ds(0, 2 * BS * (uly_n - 1) // uly_n), :]
    wait_bytes(kv_part, kv_recv)

    @pl.when(lax.rem(head, 2) == 1)
    def _():
        pl.semaphore_wait(turn, 1)

    def send_spread(i, c):
        p = blk_peer(i)
        pltpu.make_async_remote_copy(
            kv.at[:, pl.ds(pl.multiple_of(p * rows, rows), rows), :],
            table.at[pl.ds(rank * here, here)],
            spread_send, spread_recv, device_id=(p, head), device_id_type=MESH,
        ).start()
        return c

    lax.fori_loop(1, blk_n, send_spread, 0)
    table[pl.ds(rank * here, here)] = kv[:, pl.ds(pl.multiple_of(rank * rows, rows), rows), :]
    spread_part = table.at[pl.ds(0, here * (blk_n - 1))]

    @pl.when(lax.rem(head, 2) == 0)
    def _():
        wait_bytes(spread_part, spread_send)
        pl.semaphore_signal(turn, inc=1, device_id=(rank, head + 1), device_id_type=MESH)

    wait_bytes(spread_part, spread_recv)

    my_share = pl.ds(pl.multiple_of(rank * rows, rows), rows)

    def pick(half, p, s):
        block = p * here + own_last(half)
        stage[half, s, p] = table[chosen_ref[head, s, block]]

    def send_ask(n, c):
        part = lax.div(n, blk_n - 1)
        half, s = lax.div(part, 2), lax.rem(part, 2)
        p = blk_peer(lax.rem(n, blk_n - 1) + 1)
        pick(half, p, s)
        pltpu.make_async_remote_copy(
            stage.at[half, s, p], routed.at[half, s, my_share, :],
            ask_send, ask_recv.at[half, s], device_id=(p, head), device_id_type=MESH,
        ).start()
        return c

    lax.fori_loop(0, 2 * here * (blk_n - 1), send_ask, 0)
    for half in range(here):
        for s in range(2):
            pick(half, rank, s)
            routed[half, s, my_share, :] = stage[half, s, rank]

    own_q.wait()
    wait_bytes(qh.at[pl.ds(0, span - tok), :], q_recv)

    def queries(row, gh):
        return jnp.concatenate(
            [qh[pl.ds(row, tok), pl.ds(pl.multiple_of((gh * half_g + g) * HD, HD), HD)] for g in range(half_g)], axis=0)

    contract = (((1,), (1,)), ((), ()))
    ones = jnp.ones((BS, HD), jnp.bfloat16)

    def own_step(i, c):
        b = lax.div(i, 2)
        gh = lax.rem(i, 2)
        for part in range(per):
            q = queries(pl.multiple_of(b * BS + part * tok, tok), gh)
            n = (part + 1) * tok
            scores = lax.dot_general(q, kv[b, 0:n, :], contract, preferred_element_type=jnp.float32)
            r = lax.rem(lax.broadcasted_iota(jnp.int32, (half_g * tok, tok), 0), tok)
            k = lax.broadcasted_iota(jnp.int32, (half_g * tok, tok), 1)
            diag = jnp.where(k <= r, scores[:, n - tok:], -jnp.inf)
            if part:
                scores = jnp.concatenate([scores[:, : n - tok], diag], axis=1)
            else:
                scores = diag
            top = jnp.max(scores, axis=1, keepdims=True)
            weights = jnp.exp2(scores * factor - top * factor).astype(jnp.bfloat16)
            v1 = jnp.concatenate([kv[b, BS:BS + n, :], ones[:n]], axis=1)
            own_acc[b, part, gh] = jnp.dot(weights, v1, preferred_element_type=jnp.float32)
            own_top[b, part, gh] = jnp.broadcast_to(top, (half_g * tok, HD))
        return c

    lax.fori_loop(0, here * 2, own_step, 0)

    def routed_step(n, c):
        quarter = lax.div(n, per)
        half, s = lax.div(quarter, 2), lax.rem(quarter, 2)
        b = own_last(half)
        turn_of = lax.rem(n, per)
        part = jnp.where(turn_of == 0, lax.rem(seat + 2, per), jnp.where(
            turn_of == 1, per - 1 - seat, jnp.where(turn_of == 2, seat + 1 - 2 * lax.rem(seat, 2), seat)))

        @pl.when(lax.rem(n, per) == 0)
        def _():
            wait_bytes(table.at[pl.ds(0, blk_n - 1)], ask_recv.at[half, s])

        block = rank * here + b
        usable = chosen_ref[head, s, block] < block
        row = pl.multiple_of(b * BS + part * tok, tok)

        v1 = jnp.concatenate([routed[half, s, BS:, :], ones], axis=1)
        chains = [(j // 1, (j % 1) * 4 * tok, j * 4) for j in range(2)]

        def heads(g0):
            return jnp.concatenate([qh[pl.ds(row, tok), (g0 + g) * HD:(g0 + g + 1) * HD] for g in range(4)], axis=0)

        def score(chain):
            return lax.dot_general(heads(chain[2]), routed[half, s, 0:BS, :], contract, preferred_element_type=jnp.float32)

        def one(chain, scores):
            gh, r0, g0 = chain
            rr = slice(r0, r0 + 4 * tok)
            before = own_top[b, part, gh, rr]
            peak = jnp.broadcast_to(jnp.max(scores, axis=1, keepdims=True), before.shape)
            top = jnp.maximum(before, jnp.where(usable, peak, NEG))
            shift = jnp.where(usable, top * factor, jnp.inf)
            weights = jnp.exp2(scores * factor - jnp.concatenate([shift] * (BS // HD), axis=1)).astype(jnp.bfloat16)
            alpha = jnp.exp2((before - top) * factor)
            acc = own_acc[b, part, gh, rr] * jnp.concatenate([alpha, alpha], axis=1)
            return acc + jnp.dot(weights, v1, preferred_element_type=jnp.float32), top

        def run():
            out = []
            if True:
                nxt = score(chains[0])
                for i, ch in enumerate(chains):
                    cur = nxt
                    if i + 1 < len(chains):
                        nxt = score(chains[i + 1])
                    out.append((ch, *one(ch, cur)))
            else:
                out = [(ch, *one(ch, score(ch))) for ch in chains]
            return out

        @pl.when(s == 0)
        def _():
            for (gh, r0, g0), acc, top in run():
                own_acc[b, part, gh, r0:r0 + 4 * tok] = acc
                own_top[b, part, gh, r0:r0 + 4 * tok] = top

        @pl.when(s == 1)
        def _():
            for (gh, r0, g0), acc, top in run():
                result = (acc[:, :HD] / acc[:, HD:]).astype(jnp.bfloat16)
                for g in range(4):
                    outh[pl.ds(row, tok), (g0 + g) * HD:(g0 + g + 1) * HD] = result[g * tok:(g + 1) * tok]

        p = b * per + part
        src = outh.at[pl.ds(row, tok), :]
        dst = out_ref.at[:, pl.ds(pl.multiple_of(head * width, width), width)]

        @pl.when((s == 1) & (p != head))
        def _():
            pltpu.make_async_remote_copy(
                src, dst, out_send, out_recv, device_id=(rank, p), device_id_type=MESH).start()

        @pl.when((s == 1) & (p == head))
        def _():
            pltpu.make_async_copy(src, dst, self_sem.at[3]).start()

        return c

    lax.fori_loop(0, 2 * here * per, routed_step, 0)

    pltpu.make_async_copy(
        outh.at[pl.ds(0, tok), :], out_ref.at[:, pl.ds(0, width)], self_sem.at[3]).wait()
    wait_bytes(kv_part, kv_send)
    wait_bytes(qh.at[pl.ds(0, span - tok), :], q_send)

    @pl.when(lax.rem(head, 2) == 1)
    def _():
        wait_bytes(spread_part, spread_send)

    wait_bytes(stage.at[:, :, pl.ds(0, blk_n - 1)], ask_send)
    wait_bytes(qh.at[pl.ds(0, span - tok), :], out_send)
    wait_bytes(qh.at[pl.ds(0, span - tok), :], out_recv)


def solution(mesh):
    blk_n, uly_n = mesh.shape["blk"], mesh.shape["uly"]
    x_n = 4 if blk_n % 4 == 0 else 1

    def local(queries, keys, values, chosen):
        tok = queries.shape[0]
        span = tok * uly_n
        here = span // BS
        rows = 2 * BS // blk_n
        per = BS // tok
        bf = jnp.bfloat16
        any_spec = pl.BlockSpec(memory_space=pl.ANY)
        hbm_spec = pl.BlockSpec(memory_space=pltpu.HBM)
        dma = pltpu.SemaphoreType.DMA
        return pl.pallas_call(
            functools.partial(kernel, blk_n, uly_n, x_n),
            out_shape=jax.ShapeDtypeStruct(queries.shape, bf),
            in_specs=[hbm_spec, hbm_spec, hbm_spec, pl.BlockSpec(memory_space=pltpu.SMEM)],
            out_specs=any_spec,
            scratch_shapes=[
                pltpu.VMEM((span, GROUP * HD), bf),
                pltpu.VMEM((here, 2 * BS, HD), bf),
                pltpu.VMEM((blk_n * here, rows, HD), bf),
                pltpu.VMEM((here, 2, blk_n, rows, HD), bf),
                pltpu.VMEM((here, 2, 2 * BS, HD), bf),
                pltpu.VMEM((here, per, 2, GROUP // 2 * tok, 2 * HD), jnp.float32),
                pltpu.VMEM((here, per, 2, GROUP // 2 * tok, HD), jnp.float32),
                pltpu.VMEM((span, GROUP * HD), bf),
                dma, dma, dma, dma, dma, dma, dma, dma((here, 2)), dma, dma, dma((4,)),
                pltpu.SemaphoreType.REGULAR,
            ],
            compiler_params=pltpu.CompilerParams(
                collective_id=0, has_side_effects=True, vmem_limit_bytes=36 * 2**20),
        )(*[pltpu.with_memory_space_constraint(a, pltpu.HBM) for a in (queries, keys, values)], chosen.transpose(1, 2, 0))

    placed = P(("blk", "uly"), None)
    return jax.shard_map(
        local, mesh=mesh, in_specs=(placed, placed, placed, P()), out_specs=placed, check_vma=False)
```

```python
import functools

import jax
import jax.numpy as jnp
from jax import lax
from jax.experimental import pallas as pl
from jax.experimental.pallas import tpu as pltpu
from jax.sharding import PartitionSpec as P

BS = 512
HD = 128
GROUP = 8
EARLY = 4
LOG2E = 1.4426950408889634
NEG = -3.0e38
MESH = pl.DeviceIdType.MESH


def kernel(
    blk_n, uly_n, x_n,
    q_ref, k_ref, v_ref, ids_ref,
    out_ref,
    chosen_ref,
    qh, kv, table, stage, routed, own_acc, own_top, outh,
    kv_send, kv_recv, q_send, q_recv, spread_send, spread_recv, ask_send, ask_recv, out_send, out_recv, self_sem, turn,
):
    rank = lax.axis_index("blk")
    head = lax.axis_index("uly")
    tok = q_ref.shape[0]
    width = GROUP * HD
    span = uly_n * tok
    here = span // BS
    per = BS // tok
    rows = 2 * BS // blk_n
    half_g = GROUP // 2
    z_n = blk_n // x_n
    factor = HD ** (-0.5) * LOG2E
    home = lax.div(head, per)
    seat = lax.rem(head, per)

    def own_last(half):
        return jnp.where(half == here - 1, home, here - 1 - home)

    my_z, my_x = lax.div(rank, x_n), lax.rem(rank, x_n)
    xs = [lax.rem(my_x + dx, x_n) for dx in range(x_n)]

    def share_of(p):
        return pl.ds(pl.multiple_of(lax.rem(p, 2) * BS + lax.div(p, 2) * rows, rows), rows)

    def for_blk(action, columns=xs, last=xs[1:]):
        def at(i, c):
            k = z_n - 1 - i
            odd = lax.rem(k, 2)
            step = lax.div(k + 1, 2)
            z = lax.rem(my_z + z_n + step * (2 * odd - 1), z_n)
            action(i, [z * x_n + x for x in columns])
            return c

        lax.fori_loop(0, z_n - 1, at, 0)
        action(z_n - 1, [my_z * x_n + x for x in last])

    def uly_peer(i):
        return lax.rem(head + i, uly_n)

    ids = pltpu.make_async_copy(ids_ref, chosen_ref, self_sem.at[4])
    ids.start()

    barrier = pltpu.get_barrier_semaphore()

    def greet_uly(i, c):
        pl.semaphore_signal(barrier, inc=1, device_id=(rank, uly_peer(i)), device_id_type=MESH)
        return c

    def greet_blk(i, peers):
        for p in peers:
            pl.semaphore_signal(barrier, inc=1, device_id=(p, head), device_id_type=MESH)

    lax.fori_loop(1, uly_n, greet_uly, 0)
    for_blk(greet_blk)
    pl.semaphore_wait(barrier, uly_n + blk_n - 2)

    my_block = home
    my_row = pl.multiple_of(seat * tok, tok)
    my_rows = pl.ds(my_row, tok)
    my_rows_v = pl.ds(pl.multiple_of(my_row + BS, tok), tok)

    def send_kv(parity, kind):
        src, dst_rows = ((k_ref, my_rows), (v_ref, my_rows_v))[kind]

        def at(i, c):
            p = 2 * lax.rem(lax.div(head, 2) + i, uly_n // 2) + parity

            @pl.when(p != head)
            def _():
                pltpu.make_async_remote_copy(
                    src.at[:, pl.ds(pl.multiple_of(p * HD, HD), HD)], kv.at[my_block, dst_rows, :],
                    kv_send, kv_recv.at[kind], device_id=(rank, p), device_id_type=MESH,
                ).start()

            return c

        lax.fori_loop(0, uly_n // 2, at, 0)

    for parity in range(2):
        for kind in range(2):
            send_kv(parity, kind)
    own_cols = pl.ds(pl.multiple_of(head * HD, HD), HD)
    own_k = pltpu.make_async_copy(k_ref.at[:, own_cols], kv.at[my_block, my_rows, :], self_sem.at[0])
    own_v = pltpu.make_async_copy(v_ref.at[:, own_cols], kv.at[my_block, my_rows_v, :], self_sem.at[1])
    own_k.start()
    own_v.start()

    def send_q(i, c):
        p = uly_peer(i)
        pltpu.make_async_remote_copy(
            q_ref.at[:, pl.ds(pl.multiple_of(p * width, width), width)],
            qh.at[pl.ds(pl.multiple_of(head * tok, tok), tok), :],
            q_send, q_recv, device_id=(rank, p), device_id_type=MESH,
        ).start()
        return c

    lax.fori_loop(1, uly_n, send_q, 0)
    own_q = pltpu.make_async_copy(
        q_ref.at[:, pl.ds(pl.multiple_of(head * width, width), width)],
        qh.at[pl.ds(pl.multiple_of(head * tok, tok), tok), :], self_sem.at[2])
    own_q.start()

    def wait_bytes(ref, sem):
        pltpu.make_async_copy(ref, ref, sem).wait()

    kv_part = kv.at[:, pl.ds(0, 2 * BS * (uly_n - 1) // uly_n), :]
    half_part = kv.at[:, pl.ds(0, BS * (uly_n - 1) // uly_n), :]

    @pl.when(lax.rem(head, 2) == 1)
    def _():
        pl.semaphore_wait(turn, 1)

    def spread(kind, early):
        def send(i, peers):
            for p in peers:
                @pl.when(p != rank)
                def _():
                    pltpu.make_async_remote_copy(
                        kv.at[:, share_of(p), :], table.at[pl.ds(rank * here, here)],
                        spread_send.at[jnp.where(i < early, 0, 1)], spread_recv,
                        device_id=(p, head), device_id_type=MESH,
                    ).start()

        for_blk(send, range(kind, x_n, 2), range(kind, x_n, 2))

    own_k.wait()
    wait_bytes(half_part, kv_recv.at[0])
    spread(0, z_n - 1)
    own_v.wait()
    wait_bytes(half_part, kv_recv.at[1])
    spread(1, EARLY)
    table[pl.ds(rank * here, here)] = kv[:, share_of(rank), :]
    spread_part = table.at[pl.ds(0, here * (blk_n - 1))]

    @pl.when(lax.rem(head, 2) == 0)
    def _():
        wait_bytes(table.at[pl.ds(0, here * 2 * (z_n - 1 + EARLY))], spread_send.at[0])
        pl.semaphore_signal(turn, inc=1, device_id=(rank, head + 1), device_id_type=MESH)

    wait_bytes(spread_part, spread_recv)

    ids.wait()
    my_share = share_of(rank)

    def pick(half, p, s):
        block = p * here + own_last(half)
        stage[half, s, p] = table[chosen_ref[head, s, block]]

    def send_asks(n, c):
        half, s = lax.div(n, 2), lax.rem(n, 2)

        def send_ask(i, peers):
            for p in peers:
                pick(half, p, s)
            for p in peers:
                pltpu.make_async_remote_copy(
                    stage.at[half, s, p], routed.at[half, s, my_share, :],
                    ask_send, ask_recv.at[half, s], device_id=(p, head), device_id_type=MESH,
                ).start()

        for_blk(send_ask)
        return c

    lax.fori_loop(0, 2 * here, send_asks, 0)
    for half in range(here):
        for s in range(2):
            pick(half, rank, s)
            routed[half, s, my_share, :] = stage[half, s, rank]

    own_q.wait()
    wait_bytes(qh.at[pl.ds(0, span - tok), :], q_recv)

    def queries(row, gh):
        return jnp.concatenate(
            [qh[pl.ds(row, tok), pl.ds(pl.multiple_of((gh * half_g + g) * HD, HD), HD)] for g in range(half_g)], axis=0)

    contract = (((1,), (1,)), ((), ()))
    ones = jnp.ones((BS, HD), jnp.bfloat16)

    def own_step(i, c):
        b = lax.div(i, 2)
        gh = lax.rem(i, 2)
        for part in range(per):
            q = queries(pl.multiple_of(b * BS + part * tok, tok), gh)
            n = (part + 1) * tok
            scores = lax.dot_general(q, kv[b, 0:n, :], contract, preferred_element_type=jnp.float32)
            r = lax.rem(lax.broadcasted_iota(jnp.int32, (half_g * tok, tok), 0), tok)
            k = lax.broadcasted_iota(jnp.int32, (half_g * tok, tok), 1)
            diag = jnp.where(k <= r, scores[:, n - tok:], -jnp.inf)
            if part:
                scores = jnp.concatenate([scores[:, : n - tok], diag], axis=1)
            else:
                scores = diag
            top = jnp.max(scores, axis=1, keepdims=True)
            weights = jnp.exp2(scores * factor - top * factor).astype(jnp.bfloat16)
            v1 = jnp.concatenate([kv[b, BS:BS + n, :], ones[:n]], axis=1)
            own_acc[b, part, gh] = jnp.dot(weights, v1, preferred_element_type=jnp.float32)
            own_top[b, part, gh] = jnp.broadcast_to(top, (half_g * tok, HD))
        return c

    lax.fori_loop(0, here * 2, own_step, 0)

    def routed_step(n, c):
        quarter = lax.div(n, per)
        half, s = lax.div(quarter, 2), lax.rem(quarter, 2)
        b = own_last(half)
        turn_of = lax.rem(n, per)
        part = jnp.where(turn_of == 0, lax.rem(seat + 2, per), jnp.where(
            turn_of == 1, per - 1 - seat, jnp.where(turn_of == 2, seat + 1 - 2 * lax.rem(seat, 2), seat)))

        @pl.when(lax.rem(n, per) == 0)
        def _():
            wait_bytes(table.at[pl.ds(0, blk_n - 1)], ask_recv.at[half, s])

        block = rank * here + b
        usable = chosen_ref[head, s, block] < block
        row = pl.multiple_of(b * BS + part * tok, tok)

        v1 = jnp.concatenate([routed[half, s, BS:, :], ones], axis=1)
        chains = [(j // 1, (j % 1) * 4 * tok, j * 4) for j in range(2)]

        def heads(g0):
            return jnp.concatenate([qh[pl.ds(row, tok), (g0 + g) * HD:(g0 + g + 1) * HD] for g in range(4)], axis=0)

        def score(chain):
            return lax.dot_general(heads(chain[2]), routed[half, s, 0:BS, :], contract, preferred_element_type=jnp.float32)

        def one(chain, scores):
            gh, r0, g0 = chain
            rr = slice(r0, r0 + 4 * tok)
            before = own_top[b, part, gh, rr]
            peak = jnp.broadcast_to(jnp.max(scores, axis=1, keepdims=True), before.shape)
            top = jnp.maximum(before, jnp.where(usable, peak, NEG))
            shift = jnp.where(usable, top * factor, jnp.inf)
            weights = jnp.exp2(scores * factor - jnp.concatenate([shift] * (BS // HD), axis=1)).astype(jnp.bfloat16)
            alpha = jnp.exp2((before - top) * factor)
            acc = own_acc[b, part, gh, rr] * jnp.concatenate([alpha, alpha], axis=1)
            return acc + jnp.dot(weights, v1, preferred_element_type=jnp.float32), top

        def run():
            out = []
            if True:
                nxt = score(chains[0])
                for i, ch in enumerate(chains):
                    cur = nxt
                    if i + 1 < len(chains):
                        nxt = score(chains[i + 1])
                    out.append((ch, *one(ch, cur)))
            else:
                out = [(ch, *one(ch, score(ch))) for ch in chains]
            return out

        @pl.when(s == 0)
        def _():
            for (gh, r0, g0), acc, top in run():
                own_acc[b, part, gh, r0:r0 + 4 * tok] = acc
                own_top[b, part, gh, r0:r0 + 4 * tok] = top

        @pl.when(s == 1)
        def _():
            for (gh, r0, g0), acc, top in run():
                result = (acc[:, :HD] / acc[:, HD:]).astype(jnp.bfloat16)
                for g in range(4):
                    outh[pl.ds(row, tok), (g0 + g) * HD:(g0 + g + 1) * HD] = result[g * tok:(g + 1) * tok]

        p = b * per + part
        src = outh.at[pl.ds(row, tok), :]
        dst = out_ref.at[:, pl.ds(pl.multiple_of(head * width, width), width)]

        @pl.when((s == 1) & (p != head))
        def _():
            pltpu.make_async_remote_copy(
                src, dst, out_send, out_recv, device_id=(rank, p), device_id_type=MESH).start()

        @pl.when((s == 1) & (p == head))
        def _():
            pltpu.make_async_copy(src, dst, self_sem.at[3]).start()

        return c

    lax.fori_loop(0, 2 * here * per, routed_step, 0)

    pltpu.make_async_copy(
        outh.at[pl.ds(0, tok), :], out_ref.at[:, pl.ds(0, width)], self_sem.at[3]).wait()
    wait_bytes(kv_part, kv_send)
    wait_bytes(qh.at[pl.ds(0, span - tok), :], q_send)

    @pl.when(lax.rem(head, 2) == 1)
    def _():
        wait_bytes(table.at[pl.ds(0, here * 2 * (z_n - 1 + EARLY))], spread_send.at[0])

    wait_bytes(table.at[pl.ds(0, here * (blk_n - 1 - 2 * (z_n - 1 + EARLY)))], spread_send.at[1])

    wait_bytes(stage.at[:, :, pl.ds(0, blk_n - 1)], ask_send)
    wait_bytes(qh.at[pl.ds(0, span - tok), :], out_send)
    wait_bytes(qh.at[pl.ds(0, span - tok), :], out_recv)


def solution(mesh):
    blk_n, uly_n = mesh.shape["blk"], mesh.shape["uly"]
    x_n = 4 if blk_n % 4 == 0 else 1

    def local(queries, keys, values, chosen):
        tok = queries.shape[0]
        span = tok * uly_n
        here = span // BS
        rows = 2 * BS // blk_n
        per = BS // tok
        bf = jnp.bfloat16
        any_spec = pl.BlockSpec(memory_space=pl.ANY)
        hbm_spec = pl.BlockSpec(memory_space=pltpu.HBM)
        dma = pltpu.SemaphoreType.DMA
        return pl.pallas_call(
            functools.partial(kernel, blk_n, uly_n, x_n),
            out_shape=jax.ShapeDtypeStruct(queries.shape, bf),
            in_specs=[hbm_spec] * 4,
            out_specs=any_spec,
            scratch_shapes=[
                pltpu.SMEM((chosen.shape[1], chosen.shape[2], chosen.shape[0]), jnp.int32),
                pltpu.VMEM((span, GROUP * HD), bf),
                pltpu.VMEM((here, 2 * BS, HD), bf),
                pltpu.VMEM((blk_n * here, rows, HD), bf),
                pltpu.VMEM((here, 2, blk_n, rows, HD), bf),
                pltpu.VMEM((here, 2, 2 * BS, HD), bf),
                pltpu.VMEM((here, per, 2, GROUP // 2 * tok, 2 * HD), jnp.float32),
                pltpu.VMEM((here, per, 2, GROUP // 2 * tok, HD), jnp.float32),
                pltpu.VMEM((span, GROUP * HD), bf),
                dma, dma((2,)), dma, dma, dma((2,)), dma, dma, dma((here, 2)), dma, dma, dma((5,)),
                pltpu.SemaphoreType.REGULAR,
            ],
            compiler_params=pltpu.CompilerParams(
                collective_id=0, has_side_effects=True, vmem_limit_bytes=36 * 2**20),
        )(*[pltpu.with_memory_space_constraint(a, pltpu.HBM) for a in (queries, keys, values, chosen.transpose(1, 2, 0))])

    placed = P(("blk", "uly"), None)
    return jax.shard_map(
        local, mesh=mesh, in_specs=(placed, placed, placed, P()), out_specs=placed, check_vma=False)
```

```python
import functools

import jax
import jax.numpy as jnp
from jax import lax
from jax.experimental import pallas as pl
from jax.experimental.pallas import tpu as pltpu
from jax.sharding import PartitionSpec as P

BS = 512
HD = 128
GROUP = 8
EARLY = 4
LOG2E = 1.4426950408889634
NEG = -3.0e38
MESH = pl.DeviceIdType.MESH


def kernel(
    blk_n, uly_n, x_n,
    q_ref, k_ref, v_ref, ids_ref,
    out_ref,
    chosen_ref,
    qh, kv, table, stage, routed, own_acc, own_top, outh,
    kv_send, kv_recv, q_send, q_recv, spread_send, spread_recv, ask_send, ask_recv, out_send, out_recv, self_sem, turn, heard,
):
    rank = lax.axis_index("blk")
    head = lax.axis_index("uly")
    tok = q_ref.shape[0]
    width = GROUP * HD
    span = uly_n * tok
    here = span // BS
    per = BS // tok
    rows = 2 * BS // blk_n
    half_g = GROUP // 2
    z_n = blk_n // x_n
    factor = HD ** (-0.5) * LOG2E
    home = lax.div(head, per)
    seat = lax.rem(head, per)

    def own_last(half):
        return jnp.where(half == here - 1, home, here - 1 - home)

    my_z, my_x = lax.div(rank, x_n), lax.rem(rank, x_n)
    xs = [lax.rem(my_x + dx, x_n) for dx in range(x_n)]

    def share_of(p):
        kind = lax.rem(lax.div(p, x_n) + p, 2)
        return pl.ds(pl.multiple_of(kind * BS + lax.div(p, 2) * rows, rows), rows)

    def for_blk(action, columns=lambda z: xs, last=lambda z: xs[1:]):
        def at(i, c):
            k = z_n - 1 - i
            odd = lax.rem(k, 2)
            step = lax.div(k + 1, 2)
            z = lax.rem(my_z + z_n + step * (2 * odd - 1), z_n)
            action(i, [z * x_n + x for x in columns(z)])
            return c

        lax.fori_loop(0, z_n - 1, at, 0)
        action(z_n - 1, [my_z * x_n + x for x in last(my_z)])

    def uly_peer(i):
        return lax.rem(head + i, uly_n)

    ids = pltpu.make_async_copy(ids_ref, chosen_ref, self_sem.at[4])
    ids.start()

    barrier = pltpu.get_barrier_semaphore()

    def greet_uly(i, c):
        pl.semaphore_signal(barrier, inc=1, device_id=(rank, uly_peer(i)), device_id_type=MESH)
        return c

    def greet_blk(i, peers):
        for p in peers:
            pl.semaphore_signal(barrier, inc=1, device_id=(p, head), device_id_type=MESH)

    lax.fori_loop(1, uly_n, greet_uly, 0)
    for_blk(greet_blk, lambda z: [my_x])
    pl.semaphore_wait(barrier, uly_n + z_n + x_n - 3)

    my_block = home
    my_row = pl.multiple_of(seat * tok, tok)
    my_rows = pl.ds(my_row, tok)
    my_rows_v = pl.ds(pl.multiple_of(my_row + BS, tok), tok)

    def send_kv(parity, kind):
        src, dst_rows = ((k_ref, my_rows), (v_ref, my_rows_v))[kind]

        def at(i, c):
            p = 2 * lax.rem(lax.div(head, 2) + i, uly_n // 2) + parity

            @pl.when(p != head)
            def _():
                pltpu.make_async_remote_copy(
                    src.at[:, pl.ds(pl.multiple_of(p * HD, HD), HD)], kv.at[my_block, dst_rows, :],
                    kv_send, kv_recv.at[kind], device_id=(rank, p), device_id_type=MESH,
                ).start()

            return c

        lax.fori_loop(0, uly_n // 2, at, 0)

    for parity in range(2):
        for kind in range(2):
            send_kv(parity, kind)
    own_cols = pl.ds(pl.multiple_of(head * HD, HD), HD)
    own_k = pltpu.make_async_copy(k_ref.at[:, own_cols], kv.at[my_block, my_rows, :], self_sem.at[0])
    own_v = pltpu.make_async_copy(v_ref.at[:, own_cols], kv.at[my_block, my_rows_v, :], self_sem.at[1])
    own_k.start()
    own_v.start()

    for x in xs[1:]:
        pl.semaphore_signal(heard, inc=1, device_id=(my_z * x_n + x, head), device_id_type=MESH)

    def send_q(i, c):
        p = uly_peer(i)
        pltpu.make_async_remote_copy(
            q_ref.at[:, pl.ds(pl.multiple_of(p * width, width), width)],
            qh.at[pl.ds(pl.multiple_of(head * tok, tok), tok), :],
            q_send, q_recv, device_id=(rank, p), device_id_type=MESH,
        ).start()
        return c

    lax.fori_loop(1, uly_n, send_q, 0)
    own_q = pltpu.make_async_copy(
        q_ref.at[:, pl.ds(pl.multiple_of(head * width, width), width)],
        qh.at[pl.ds(pl.multiple_of(head * tok, tok), tok), :], self_sem.at[2])
    own_q.start()

    def wait_bytes(ref, sem):
        pltpu.make_async_copy(ref, ref, sem).wait()

    kv_part = kv.at[:, pl.ds(0, 2 * BS * (uly_n - 1) // uly_n), :]
    half_part = kv.at[:, pl.ds(0, BS * (uly_n - 1) // uly_n), :]

    @pl.when(lax.rem(head, 2) == 1)
    def _():
        pl.semaphore_wait(turn, 1)

    def spread(kind, early):
        def send(i, peers):
            for p in peers:
                @pl.when(p != rank)
                def _():
                    pltpu.make_async_remote_copy(
                        kv.at[:, share_of(p), :], table.at[pl.ds(rank * here, here)],
                        spread_send.at[jnp.where(i < early, 0, 1)], spread_recv,
                        device_id=(p, head), device_id_type=MESH,
                    ).start()

        def columns(z):
            first = my_x + lax.rem(kind + z + my_x, 2)
            return [lax.rem(first + dx, x_n) for dx in range(0, x_n, 2)]

        for_blk(send, columns, columns)

    pl.semaphore_wait(heard, x_n - 1)
    own_k.wait()
    wait_bytes(half_part, kv_recv.at[0])
    spread(0, z_n - 1)
    own_v.wait()
    wait_bytes(half_part, kv_recv.at[1])
    spread(1, EARLY)
    table[pl.ds(rank * here, here)] = kv[:, share_of(rank), :]
    spread_part = table.at[pl.ds(0, here * (blk_n - 1))]

    @pl.when(lax.rem(head, 2) == 0)
    def _():
        wait_bytes(table.at[pl.ds(0, here * 2 * (z_n - 1 + EARLY))], spread_send.at[0])
        pl.semaphore_signal(turn, inc=1, device_id=(rank, head + 1), device_id_type=MESH)

    wait_bytes(spread_part, spread_recv)

    ids.wait()
    my_share = share_of(rank)

    def pick(half, p, s):
        block = p * here + own_last(half)
        stage[half, s, p] = table[chosen_ref[head, s, block]]

    def send_asks(n, c):
        half, s = lax.div(n, 2), lax.rem(n, 2)

        def send_ask(i, peers):
            for p in peers:
                pick(half, p, s)
            for p in peers:
                pltpu.make_async_remote_copy(
                    stage.at[half, s, p], routed.at[half, s, my_share, :],
                    ask_send, ask_recv.at[half, s], device_id=(p, head), device_id_type=MESH,
                ).start()

        for_blk(send_ask)
        return c

    lax.fori_loop(0, 2 * here, send_asks, 0)
    for half in range(here):
        for s in range(2):
            pick(half, rank, s)
            routed[half, s, my_share, :] = stage[half, s, rank]

    own_q.wait()
    wait_bytes(qh.at[pl.ds(0, span - tok), :], q_recv)

    def queries(row, gh):
        return jnp.concatenate(
            [qh[pl.ds(row, tok), pl.ds(pl.multiple_of((gh * half_g + g) * HD, HD), HD)] for g in range(half_g)], axis=0)

    contract = (((1,), (1,)), ((), ()))
    ones = jnp.ones((BS, HD), jnp.bfloat16)

    def own_step(i, c):
        b = lax.div(i, 2)
        gh = lax.rem(i, 2)
        for part in range(per):
            q = queries(pl.multiple_of(b * BS + part * tok, tok), gh)
            n = (part + 1) * tok
            scores = lax.dot_general(q, kv[b, 0:n, :], contract, preferred_element_type=jnp.float32)
            r = lax.rem(lax.broadcasted_iota(jnp.int32, (half_g * tok, tok), 0), tok)
            k = lax.broadcasted_iota(jnp.int32, (half_g * tok, tok), 1)
            diag = jnp.where(k <= r, scores[:, n - tok:], -jnp.inf)
            if part:
                scores = jnp.concatenate([scores[:, : n - tok], diag], axis=1)
            else:
                scores = diag
            top = jnp.max(scores, axis=1, keepdims=True)
            weights = jnp.exp2(scores * factor - top * factor).astype(jnp.bfloat16)
            v1 = jnp.concatenate([kv[b, BS:BS + n, :], ones[:n]], axis=1)
            own_acc[b, part, gh] = jnp.dot(weights, v1, preferred_element_type=jnp.float32)
            own_top[b, part, gh] = jnp.broadcast_to(top, (half_g * tok, HD))
        return c

    lax.fori_loop(0, here * 2, own_step, 0)

    def routed_step(n, c):
        quarter = lax.div(n, per)
        half, s = lax.div(quarter, 2), lax.rem(quarter, 2)
        b = own_last(half)
        turn_of = lax.rem(n, per)
        part = jnp.where(turn_of == 0, lax.rem(seat + 2, per), jnp.where(
            turn_of == 1, per - 1 - seat, jnp.where(turn_of == 2, seat + 1 - 2 * lax.rem(seat, 2), seat)))

        @pl.when(lax.rem(n, per) == 0)
        def _():
            wait_bytes(table.at[pl.ds(0, blk_n - 1)], ask_recv.at[half, s])

        block = rank * here + b
        usable = chosen_ref[head, s, block] < block
        row = pl.multiple_of(b * BS + part * tok, tok)

        v1 = jnp.concatenate([routed[half, s, BS:, :], ones], axis=1)
        chains = [(j // 1, (j % 1) * 4 * tok, j * 4) for j in range(2)]

        def heads(g0):
            return jnp.concatenate([qh[pl.ds(row, tok), (g0 + g) * HD:(g0 + g + 1) * HD] for g in range(4)], axis=0)

        def score(chain):
            return lax.dot_general(heads(chain[2]), routed[half, s, 0:BS, :], contract, preferred_element_type=jnp.float32)

        def one(chain, scores):
            gh, r0, g0 = chain
            rr = slice(r0, r0 + 4 * tok)
            before = own_top[b, part, gh, rr]
            peak = jnp.broadcast_to(jnp.max(scores, axis=1, keepdims=True), before.shape)
            top = jnp.maximum(before, jnp.where(usable, peak, NEG))
            shift = jnp.where(usable, top * factor, jnp.inf)
            weights = jnp.exp2(scores * factor - jnp.concatenate([shift] * (BS // HD), axis=1)).astype(jnp.bfloat16)
            alpha = jnp.exp2((before - top) * factor)
            acc = own_acc[b, part, gh, rr] * jnp.concatenate([alpha, alpha], axis=1)
            return acc + jnp.dot(weights, v1, preferred_element_type=jnp.float32), top

        def run():
            out = []
            if True:
                nxt = score(chains[0])
                for i, ch in enumerate(chains):
                    cur = nxt
                    if i + 1 < len(chains):
                        nxt = score(chains[i + 1])
                    out.append((ch, *one(ch, cur)))
            else:
                out = [(ch, *one(ch, score(ch))) for ch in chains]
            return out

        @pl.when(s == 0)
        def _():
            for (gh, r0, g0), acc, top in run():
                own_acc[b, part, gh, r0:r0 + 4 * tok] = acc
                own_top[b, part, gh, r0:r0 + 4 * tok] = top

        @pl.when(s == 1)
        def _():
            for (gh, r0, g0), acc, top in run():
                result = (acc[:, :HD] / acc[:, HD:]).astype(jnp.bfloat16)
                for g in range(4):
                    outh[pl.ds(row, tok), (g0 + g) * HD:(g0 + g + 1) * HD] = result[g * tok:(g + 1) * tok]

        p = b * per + part
        src = outh.at[pl.ds(row, tok), :]
        dst = out_ref.at[:, pl.ds(pl.multiple_of(head * width, width), width)]

        @pl.when((s == 1) & (p != head))
        def _():
            pltpu.make_async_remote_copy(
                src, dst, out_send, out_recv, device_id=(rank, p), device_id_type=MESH).start()

        @pl.when((s == 1) & (p == head))
        def _():
            pltpu.make_async_copy(src, dst, self_sem.at[3]).start()

        return c

    lax.fori_loop(0, 2 * here * per, routed_step, 0)

    pltpu.make_async_copy(
        outh.at[pl.ds(0, tok), :], out_ref.at[:, pl.ds(0, width)], self_sem.at[3]).wait()
    wait_bytes(kv_part, kv_send)
    wait_bytes(qh.at[pl.ds(0, span - tok), :], q_send)

    @pl.when(lax.rem(head, 2) == 1)
    def _():
        wait_bytes(table.at[pl.ds(0, here * 2 * (z_n - 1 + EARLY))], spread_send.at[0])

    wait_bytes(table.at[pl.ds(0, here * (blk_n - 1 - 2 * (z_n - 1 + EARLY)))], spread_send.at[1])

    wait_bytes(stage.at[:, :, pl.ds(0, blk_n - 1)], ask_send)
    wait_bytes(qh.at[pl.ds(0, span - tok), :], out_send)
    wait_bytes(qh.at[pl.ds(0, span - tok), :], out_recv)


def solution(mesh):
    blk_n, uly_n = mesh.shape["blk"], mesh.shape["uly"]
    x_n = 4 if blk_n % 4 == 0 else 1

    def local(queries, keys, values, chosen):
        tok = queries.shape[0]
        span = tok * uly_n
        here = span // BS
        rows = 2 * BS // blk_n
        per = BS // tok
        bf = jnp.bfloat16
        any_spec = pl.BlockSpec(memory_space=pl.ANY)
        hbm_spec = pl.BlockSpec(memory_space=pltpu.HBM)
        dma = pltpu.SemaphoreType.DMA
        return pl.pallas_call(
            functools.partial(kernel, blk_n, uly_n, x_n),
            out_shape=jax.ShapeDtypeStruct(queries.shape, bf),
            in_specs=[hbm_spec] * 4,
            out_specs=any_spec,
            scratch_shapes=[
                pltpu.SMEM((chosen.shape[1], chosen.shape[2], chosen.shape[0]), jnp.int32),
                pltpu.VMEM((span, GROUP * HD), bf),
                pltpu.VMEM((here, 2 * BS, HD), bf),
                pltpu.VMEM((blk_n * here, rows, HD), bf),
                pltpu.VMEM((here, 2, blk_n, rows, HD), bf),
                pltpu.VMEM((here, 2, 2 * BS, HD), bf),
                pltpu.VMEM((here, per, 2, GROUP // 2 * tok, 2 * HD), jnp.float32),
                pltpu.VMEM((here, per, 2, GROUP // 2 * tok, HD), jnp.float32),
                pltpu.VMEM((span, GROUP * HD), bf),
                dma, dma((2,)), dma, dma, dma((2,)), dma, dma, dma((here, 2)), dma, dma, dma((5,)),
                pltpu.SemaphoreType.REGULAR, pltpu.SemaphoreType.REGULAR,
            ],
            compiler_params=pltpu.CompilerParams(
                collective_id=0, has_side_effects=True, vmem_limit_bytes=36 * 2**20),
        )(*[pltpu.with_memory_space_constraint(a, pltpu.HBM) for a in (queries, keys, values, chosen.transpose(1, 2, 0))])

    placed = P(("blk", "uly"), None)
    return jax.shard_map(
        local, mesh=mesh, in_specs=(placed, placed, placed, P()), out_specs=placed, check_vma=False)
```

```python
import functools

import jax
import jax.numpy as jnp
from jax import lax
from jax.experimental import pallas as pl
from jax.experimental.pallas import tpu as pltpu
from jax.sharding import PartitionSpec as P

BS = 512
HD = 128
GROUP = 8
EARLY = 4
LOG2E = 1.4426950408889634
NEG = -3.0e38
MESH = pl.DeviceIdType.MESH


def kernel(
    blk_n, uly_n, x_n,
    q_ref, k_ref, v_ref, ids_ref,
    out_ref,
    chosen_ref,
    qh, kv, table, stage, routed, own_acc, own_top, outh,
    kv_send, kv_recv, q_send, q_recv, spread_send, spread_recv, ask_send, ask_recv, out_send, out_recv, self_sem, turn, heard,
):
    rank = lax.axis_index("blk")
    head = lax.axis_index("uly")
    tok = q_ref.shape[0]
    width = GROUP * HD
    span = uly_n * tok
    here = span // BS
    per = BS // tok
    rows = 2 * BS // blk_n
    half_g = GROUP // 2
    z_n = blk_n // x_n
    factor = HD ** (-0.5) * LOG2E
    home = lax.div(head, per)
    seat = lax.rem(head, per)

    def own_last(half):
        return jnp.where(half == here - 1, home, here - 1 - home)

    my_z, my_x = lax.div(rank, x_n), lax.rem(rank, x_n)
    xs = [lax.rem(my_x + dx, x_n) for dx in range(x_n)]

    def share_of(p):
        kind = lax.rem(lax.div(p, x_n) + p, 2)
        return pl.ds(pl.multiple_of(kind * BS + lax.div(p, 2) * rows, rows), rows)

    def for_blk(action, columns=lambda z: xs, last=lambda z: xs[1:]):
        def at(i, c):
            k = z_n - 1 - i
            odd = lax.rem(k, 2)
            step = lax.div(k + 1, 2)
            z = lax.rem(my_z + z_n + step * (2 * odd - 1), z_n)
            action(i, [z * x_n + x for x in columns(z)])
            return c

        lax.fori_loop(0, z_n - 1, at, 0)
        action(z_n - 1, [my_z * x_n + x for x in last(my_z)])

    def uly_peer(i):
        return lax.rem(head + i, uly_n)

    ids = pltpu.make_async_copy(ids_ref, chosen_ref, self_sem.at[4])
    ids.start()

    barrier = pltpu.get_barrier_semaphore()

    def greet_uly(i, c):
        pl.semaphore_signal(barrier, inc=1, device_id=(rank, uly_peer(i)), device_id_type=MESH)
        return c

    def greet_blk(i, peers):
        for p in peers:
            pl.semaphore_signal(barrier, inc=1, device_id=(p, head), device_id_type=MESH)

    lax.fori_loop(1, uly_n, greet_uly, 0)
    def greet_z(k, c):
        step = lax.div(k + 1, 2) * (2 * lax.rem(k, 2) - 1)
        greet_blk(k, [lax.rem(my_z + z_n + step, z_n) * x_n + my_x])
        return c

    greet_blk(0, [my_z * x_n + x for x in xs[1:]])
    lax.fori_loop(1, z_n, greet_z, 0)
    pl.semaphore_wait(barrier, uly_n + z_n + x_n - 3)

    my_block = home
    my_row = pl.multiple_of(seat * tok, tok)
    my_rows = pl.ds(my_row, tok)
    my_rows_v = pl.ds(pl.multiple_of(my_row + BS, tok), tok)

    def send_kv(parity, kind):
        src, dst_rows = ((k_ref, my_rows), (v_ref, my_rows_v))[kind]

        def at(i, c):
            p = 2 * lax.rem(lax.div(head, 2) + i, uly_n // 2) + parity

            @pl.when(p != head)
            def _():
                pltpu.make_async_remote_copy(
                    src.at[:, pl.ds(pl.multiple_of(p * HD, HD), HD)], kv.at[my_block, dst_rows, :],
                    kv_send, kv_recv.at[kind], device_id=(rank, p), device_id_type=MESH,
                ).start()

            return c

        lax.fori_loop(0, uly_n // 2, at, 0)

    for parity in range(2):
        for kind in range(2):
            send_kv(parity, kind)
    own_cols = pl.ds(pl.multiple_of(head * HD, HD), HD)
    own_k = pltpu.make_async_copy(k_ref.at[:, own_cols], kv.at[my_block, my_rows, :], self_sem.at[0])
    own_v = pltpu.make_async_copy(v_ref.at[:, own_cols], kv.at[my_block, my_rows_v, :], self_sem.at[1])
    own_k.start()
    own_v.start()

    for x in xs[1:]:
        pl.semaphore_signal(heard, inc=1, device_id=(my_z * x_n + x, head), device_id_type=MESH)

    def send_q(i, c):
        p = uly_peer(i)
        pltpu.make_async_remote_copy(
            q_ref.at[:, pl.ds(pl.multiple_of(p * width, width), width)],
            qh.at[pl.ds(pl.multiple_of(head * tok, tok), tok), :],
            q_send, q_recv, device_id=(rank, p), device_id_type=MESH,
        ).start()
        return c

    lax.fori_loop(1, uly_n, send_q, 0)
    own_q = pltpu.make_async_copy(
        q_ref.at[:, pl.ds(pl.multiple_of(head * width, width), width)],
        qh.at[pl.ds(pl.multiple_of(head * tok, tok), tok), :], self_sem.at[2])
    own_q.start()

    def wait_bytes(ref, sem):
        pltpu.make_async_copy(ref, ref, sem).wait()

    kv_part = kv.at[:, pl.ds(0, 2 * BS * (uly_n - 1) // uly_n), :]
    half_part = kv.at[:, pl.ds(0, BS * (uly_n - 1) // uly_n), :]

    @pl.when(lax.rem(head, 2) == 1)
    def _():
        pl.semaphore_wait(turn, 1)

    def spread(kind, early):
        def send(i, peers):
            for p in peers:
                @pl.when(p != rank)
                def _():
                    pltpu.make_async_remote_copy(
                        kv.at[:, share_of(p), :], table.at[pl.ds(rank * here, here)],
                        spread_send.at[jnp.where(i < early, 0, 1)], spread_recv,
                        device_id=(p, head), device_id_type=MESH,
                    ).start()

        def columns(z):
            first = my_x + lax.rem(kind + z + my_x, 2)
            return [lax.rem(first + dx, x_n) for dx in range(0, x_n, 2)]

        for_blk(send, columns, columns)

    pl.semaphore_wait(heard, x_n - 1)
    own_k.wait()
    wait_bytes(half_part, kv_recv.at[0])
    spread(0, z_n - 1)
    own_v.wait()
    wait_bytes(half_part, kv_recv.at[1])
    spread(1, EARLY)
    table[pl.ds(rank * here, here)] = kv[:, share_of(rank), :]
    spread_part = table.at[pl.ds(0, here * (blk_n - 1))]

    @pl.when(lax.rem(head, 2) == 0)
    def _():
        wait_bytes(table.at[pl.ds(0, here * 2 * (z_n - 1 + EARLY))], spread_send.at[0])
        pl.semaphore_signal(turn, inc=1, device_id=(rank, head + 1), device_id_type=MESH)

    wait_bytes(spread_part, spread_recv)

    ids.wait()
    my_share = share_of(rank)

    def pick(half, p, s):
        block = p * here + own_last(half)
        stage[half, s, p] = table[chosen_ref[head, s, block]]

    def send_asks(n, c):
        half, s = lax.div(n, 2), lax.rem(n, 2)

        def send_ask(i, peers):
            for p in peers:
                pick(half, p, s)
            for p in peers:
                pltpu.make_async_remote_copy(
                    stage.at[half, s, p], routed.at[half, s, my_share, :],
                    ask_send, ask_recv.at[half, s], device_id=(p, head), device_id_type=MESH,
                ).start()

        for_blk(send_ask)
        return c

    lax.fori_loop(0, 2 * here, send_asks, 0)
    for half in range(here):
        for s in range(2):
            pick(half, rank, s)
            routed[half, s, my_share, :] = stage[half, s, rank]

    own_q.wait()
    wait_bytes(qh.at[pl.ds(0, span - tok), :], q_recv)

    def queries(row, gh):
        return jnp.concatenate(
            [qh[pl.ds(row, tok), pl.ds(pl.multiple_of((gh * half_g + g) * HD, HD), HD)] for g in range(half_g)], axis=0)

    contract = (((1,), (1,)), ((), ()))
    ones = jnp.ones((BS, HD), jnp.bfloat16)

    def own_step(i, c):
        b = lax.div(i, 2)
        gh = lax.rem(i, 2)
        for part in range(per):
            q = queries(pl.multiple_of(b * BS + part * tok, tok), gh)
            n = (part + 1) * tok
            scores = lax.dot_general(q, kv[b, 0:n, :], contract, preferred_element_type=jnp.float32)
            r = lax.rem(lax.broadcasted_iota(jnp.int32, (half_g * tok, tok), 0), tok)
            k = lax.broadcasted_iota(jnp.int32, (half_g * tok, tok), 1)
            diag = jnp.where(k <= r, scores[:, n - tok:], -jnp.inf)
            if part:
                scores = jnp.concatenate([scores[:, : n - tok], diag], axis=1)
            else:
                scores = diag
            top = jnp.max(scores, axis=1, keepdims=True)
            weights = jnp.exp2(scores * factor - top * factor).astype(jnp.bfloat16)
            v1 = jnp.concatenate([kv[b, BS:BS + n, :], ones[:n]], axis=1)
            own_acc[b, part, gh] = jnp.dot(weights, v1, preferred_element_type=jnp.float32)
            own_top[b, part, gh] = jnp.broadcast_to(top, (half_g * tok, HD))
        return c

    lax.fori_loop(0, here * 2, own_step, 0)

    def routed_step(n, c):
        quarter = lax.div(n, per)
        half, s = lax.div(quarter, 2), lax.rem(quarter, 2)
        b = own_last(half)
        turn_of = lax.rem(n, per)
        part = jnp.where(turn_of == 0, lax.rem(seat + 2, per), jnp.where(
            turn_of == 1, per - 1 - seat, jnp.where(turn_of == 2, seat + 1 - 2 * lax.rem(seat, 2), seat)))

        @pl.when(lax.rem(n, per) == 0)
        def _():
            wait_bytes(table.at[pl.ds(0, blk_n - 1)], ask_recv.at[half, s])

        block = rank * here + b
        usable = chosen_ref[head, s, block] < block
        row = pl.multiple_of(b * BS + part * tok, tok)

        v1 = jnp.concatenate([routed[half, s, BS:, :], ones], axis=1)
        chains = [(j // 1, (j % 1) * 4 * tok, j * 4) for j in range(2)]

        def heads(g0):
            return jnp.concatenate([qh[pl.ds(row, tok), (g0 + g) * HD:(g0 + g + 1) * HD] for g in range(4)], axis=0)

        def score(chain):
            return lax.dot_general(heads(chain[2]), routed[half, s, 0:BS, :], contract, preferred_element_type=jnp.float32)

        def one(chain, scores):
            gh, r0, g0 = chain
            rr = slice(r0, r0 + 4 * tok)
            before = own_top[b, part, gh, rr]
            peak = jnp.broadcast_to(jnp.max(scores, axis=1, keepdims=True), before.shape)
            top = jnp.maximum(before, jnp.where(usable, peak, NEG))
            shift = jnp.where(usable, top * factor, jnp.inf)
            weights = jnp.exp2(scores * factor - jnp.concatenate([shift] * (BS // HD), axis=1)).astype(jnp.bfloat16)
            alpha = jnp.exp2((before - top) * factor)
            acc = own_acc[b, part, gh, rr] * jnp.concatenate([alpha, alpha], axis=1)
            return acc + jnp.dot(weights, v1, preferred_element_type=jnp.float32), top

        def run():
            out = []
            if True:
                nxt = score(chains[0])
                for i, ch in enumerate(chains):
                    cur = nxt
                    if i + 1 < len(chains):
                        nxt = score(chains[i + 1])
                    out.append((ch, *one(ch, cur)))
            else:
                out = [(ch, *one(ch, score(ch))) for ch in chains]
            return out

        @pl.when(s == 0)
        def _():
            for (gh, r0, g0), acc, top in run():
                own_acc[b, part, gh, r0:r0 + 4 * tok] = acc
                own_top[b, part, gh, r0:r0 + 4 * tok] = top

        @pl.when(s == 1)
        def _():
            for (gh, r0, g0), acc, top in run():
                result = (acc[:, :HD] / acc[:, HD:]).astype(jnp.bfloat16)
                for g in range(4):
                    outh[pl.ds(row, tok), (g0 + g) * HD:(g0 + g + 1) * HD] = result[g * tok:(g + 1) * tok]

        p = b * per + part
        src = outh.at[pl.ds(row, tok), :]
        dst = out_ref.at[:, pl.ds(pl.multiple_of(head * width, width), width)]

        @pl.when((s == 1) & (p != head))
        def _():
            pltpu.make_async_remote_copy(
                src, dst, out_send, out_recv, device_id=(rank, p), device_id_type=MESH).start()

        @pl.when((s == 1) & (p == head))
        def _():
            pltpu.make_async_copy(src, dst, self_sem.at[3]).start()

        return c

    lax.fori_loop(0, 2 * here * per, routed_step, 0)

    pltpu.make_async_copy(
        outh.at[pl.ds(0, tok), :], out_ref.at[:, pl.ds(0, width)], self_sem.at[3]).wait()
    wait_bytes(kv_part, kv_send)
    wait_bytes(qh.at[pl.ds(0, span - tok), :], q_send)

    @pl.when(lax.rem(head, 2) == 1)
    def _():
        wait_bytes(table.at[pl.ds(0, here * 2 * (z_n - 1 + EARLY))], spread_send.at[0])

    wait_bytes(table.at[pl.ds(0, here * (blk_n - 1 - 2 * (z_n - 1 + EARLY)))], spread_send.at[1])

    wait_bytes(stage.at[:, :, pl.ds(0, blk_n - 1)], ask_send)
    wait_bytes(qh.at[pl.ds(0, span - tok), :], out_send)
    wait_bytes(qh.at[pl.ds(0, span - tok), :], out_recv)


def solution(mesh):
    blk_n, uly_n = mesh.shape["blk"], mesh.shape["uly"]
    x_n = 4 if blk_n % 4 == 0 else 1

    def local(queries, keys, values, chosen):
        tok = queries.shape[0]
        span = tok * uly_n
        here = span // BS
        rows = 2 * BS // blk_n
        per = BS // tok
        bf = jnp.bfloat16
        any_spec = pl.BlockSpec(memory_space=pl.ANY)
        hbm_spec = pl.BlockSpec(memory_space=pltpu.HBM)
        dma = pltpu.SemaphoreType.DMA
        return pl.pallas_call(
            functools.partial(kernel, blk_n, uly_n, x_n),
            out_shape=jax.ShapeDtypeStruct(queries.shape, bf),
            in_specs=[hbm_spec] * 4,
            out_specs=any_spec,
            scratch_shapes=[
                pltpu.SMEM((chosen.shape[1], chosen.shape[2], chosen.shape[0]), jnp.int32),
                pltpu.VMEM((span, GROUP * HD), bf),
                pltpu.VMEM((here, 2 * BS, HD), bf),
                pltpu.VMEM((blk_n * here, rows, HD), bf),
                pltpu.VMEM((here, 2, blk_n, rows, HD), bf),
                pltpu.VMEM((here, 2, 2 * BS, HD), bf),
                pltpu.VMEM((here, per, 2, GROUP // 2 * tok, 2 * HD), jnp.float32),
                pltpu.VMEM((here, per, 2, GROUP // 2 * tok, HD), jnp.float32),
                pltpu.VMEM((span, GROUP * HD), bf),
                dma, dma((2,)), dma, dma, dma((2,)), dma, dma, dma((here, 2)), dma, dma, dma((5,)),
                pltpu.SemaphoreType.REGULAR, pltpu.SemaphoreType.REGULAR,
            ],
            compiler_params=pltpu.CompilerParams(
                collective_id=0, has_side_effects=True, vmem_limit_bytes=36 * 2**20),
        )(*[pltpu.with_memory_space_constraint(a, pltpu.HBM) for a in (queries, keys, values, chosen.transpose(1, 2, 0))])

    placed = P(("blk", "uly"), None)
    return jax.shard_map(
        local, mesh=mesh, in_specs=(placed, placed, placed, P()), out_specs=placed, check_vma=False)
```
